32 devices in a mesh: inner: 4 (over y, x), blk: 8 (over z, core).
Axes of the slice: x: 2, y: 2, z: 4, core: 2. Of those that a mesh axis runs over, the one named last changes fastest.
Arguments:
- image_emb: float32 [768, 768], P(('inner', 'blk')), may hold values from -150 to 150
- text_emb: float32 [768, 768], P(('inner', 'blk')), may hold values from -150 to 150
- logit_scale: float32 [1], replicated, may hold values from 30 to 100
Outputs:
- mean_loss: float32 [1], replicated
- image_grad: float32 [768, 768], P(('inner', 'blk'))
- text_grad: float32 [768, 768], P(('inner', 'blk'))
The draws below stay inside these ranges and needn't reach their ends.
All inputs are finite; a program needn't handle non-finite values.
Results may differ from the reference program's by a relative error of at most 0.006.
Values may be sent and summed in bfloat16 or wider, within the bound.
A program may use at most 64 MiB of HBM per device.

```python
import jax
import jax.numpy as jnp
from jax import lax

E = 768
BATCH = 768


def embed_pair(key):
    keys = jax.random.split(jax.random.fold_in(key, 4242), 5)
    image_noise = jax.random.truncated_normal(keys[0], -5.0, 5.0, (BATCH, E), jnp.float32)
    text_noise = jax.random.truncated_normal(keys[1], -5.0, 5.0, (BATCH, E), jnp.float32)
    image_spread = jnp.exp(jax.random.uniform(keys[3], (BATCH, 1), jnp.float32) * jnp.log(10.0))
    text_spread = jnp.exp(jax.random.uniform(keys[4], (BATCH, 1), jnp.float32) * jnp.log(10.0))
    image_rows = image_noise
    text_rows = text_noise
    return (image_rows * image_spread, text_rows * text_spread)


def draw_image_emb(key, part):
    return embed_pair(key)[0]


def draw_text_emb(key, part):
    return embed_pair(key)[1]


def draw_logit_scale(key, part):
    sample = jax.random.uniform(jax.random.fold_in(key, 99), (1,), jnp.float32)
    return jnp.exp(jnp.log(30.0) + sample * jnp.log(100.0 / 30.0))


def setup_inputs(seed: int = 0) -> dict:
    splits = jax.random.split(jax.random.key(seed), 4)
    return {
        "image_emb": draw_image_emb(jax.random.fold_in(splits[3], 71), 0),
        "text_emb": draw_text_emb(jax.random.fold_in(splits[3], 71), 0),
        "logit_scale": draw_logit_scale(jax.random.fold_in(splits[3], 71), 0),
    }


EPSILON = 1e-06

def unit_rows(values):
    inverse = lax.rsqrt(lax.optimization_barrier(jnp.sum(values * values, axis=1, keepdims=True)) + EPSILON)
    return (values * inverse, inverse)

def project(gradient, direction, inverse):
    return (gradient - direction * lax.optimization_barrier(jnp.sum(gradient * direction, axis=1, keepdims=True))) * inverse

def reference(image_emb, text_emb, logit_scale):
    factor = logit_scale[0]
    image_unit, image_inverse = unit_rows(image_emb)
    text_unit, text_inverse = unit_rows(text_emb)
    image_half = image_unit.astype(jnp.bfloat16)
    text_half = text_unit.astype(jnp.bfloat16)
    count_rows = image_emb.shape[0]
    embed_width = image_emb.shape[1]
    text_blocks = text_half.reshape(16, count_rows // 16, embed_width)

    def scores(text_block):
        return factor * jnp.dot(image_half, text_block.T, preferred_element_type=jnp.float32)

    def stats_step(state, text_block):
        row_peak, row_total = state
        logits = scores(text_block)
        new_peak = jnp.maximum(row_peak, lax.optimization_barrier(jnp.max(logits, axis=1)))
        row_total = row_total * jnp.exp(row_peak - new_peak) + lax.optimization_barrier(jnp.sum(jnp.exp(logits - new_peak[:, None]), axis=1))
        col_peak = lax.optimization_barrier(jnp.max(logits, axis=0))
        col_lse = col_peak + jnp.log(lax.optimization_barrier(jnp.sum(jnp.exp(logits - col_peak[None, :]), axis=0)))
        return ((new_peak, row_total), col_lse)
    initial = (jnp.full((count_rows,), -1e+30, jnp.float32), jnp.zeros((count_rows,), jnp.float32))
    (row_peak, row_total), col_parts = lax.scan(stats_step, initial, text_blocks)
    row_lse = row_peak + jnp.log(row_total)
    col_lse = col_parts.reshape(count_rows)

    def grad_step(image_acc, inputs):
        text_block, col_block = inputs
        logits = scores(text_block)
        weights = (0.5 * factor * (jnp.exp(logits - row_lse[:, None]) + jnp.exp(logits - col_block[None, :]))).astype(jnp.bfloat16)
        image_acc = image_acc + jnp.dot(weights, text_block, preferred_element_type=jnp.float32)
        text_part = jnp.dot(weights.T, image_half, preferred_element_type=jnp.float32)
        return (image_acc, text_part)
    image_sum, text_parts = lax.scan(grad_step, jnp.zeros((count_rows, embed_width), jnp.float32), (text_blocks, col_lse.reshape(16, count_rows // 16)))
    text_sum = text_parts.reshape(count_rows, embed_width)
    diagonal = factor * lax.optimization_barrier(jnp.sum(image_half.astype(jnp.float32) * text_half.astype(jnp.float32), axis=1))
    mean_loss = (jnp.sum(row_lse - diagonal) + jnp.sum(col_lse - diagonal)) / (2.0 * count_rows)
    image_pull = image_sum - factor * text_half.astype(jnp.float32)
    text_pull = text_sum - factor * image_half.astype(jnp.float32)
    return (mean_loss.reshape(1), project(image_pull, image_unit, image_inverse), project(text_pull, text_unit, text_inverse))
```

```python
import functools

import jax
import jax.numpy as jnp
from jax import lax
from jax.experimental import pallas as pl
from jax.experimental.pallas import tpu as pltpu
from jax.sharding import PartitionSpec as P

EPSILON = 1e-06
MESH = pl.DeviceIdType.MESH


def unit_rows(values):
    inverse = lax.rsqrt(jnp.sum(values * values, axis=1, keepdims=True) + EPSILON)
    return (values * inverse, inverse)


def project(gradient, direction, inverse):
    return (gradient - direction * jnp.sum(gradient * direction, axis=1, keepdims=True)) * inverse


class Group:
    def __init__(self, me, size, device_of, sems):
        self.me, self.size, self.device_of, self.sems = me, size, device_of, sems

    def on(self, step):
        return lax.rem(self.me + step, self.size)

    def back(self, step):
        return lax.rem(self.me + self.size - step, self.size)

    def copy(self, src, dst, stage, step, to):
        send_sems, recv_sems = self.sems
        return pltpu.make_async_remote_copy(
            src_ref=src,
            dst_ref=dst,
            send_sem=send_sems.at[stage, step],
            recv_sem=recv_sems.at[stage, step],
            device_id=self.device_of(to),
            device_id_type=MESH,
        )

    def steps(self):
        return range(1, self.size)

    def start_gather(self, buf, stage):
        mine = buf.at[self.me]
        for step in self.steps():
            self.copy(mine, mine, stage, step, self.on(step)).start()

    def wait_gather(self, buf, stage):
        for step in self.steps():
            theirs = buf.at[self.back(step)]
            self.copy(theirs, theirs, stage, step, self.back(step)).wait_recv()

    def end_gather(self, buf, stage):
        mine = buf.at[self.me]
        for step in self.steps():
            self.copy(mine, mine, stage, step, self.on(step)).wait_send()

    def start_scatter(self, parts, slots, stage):
        for step in self.steps():
            to = self.on(step)
            self.copy(parts.at[to], slots.at[step], stage, step, to).start()

    def wait_scatter(self, parts, slots, stage):
        for step in self.steps():
            to = self.on(step)
            self.copy(parts.at[to], slots.at[step], stage, step, to).wait()


def as_column(row):
    size = row.shape[1]
    shape = (size, size)
    same = lax.broadcasted_iota(jnp.int32, shape, 0) == lax.broadcasted_iota(jnp.int32, shape, 1)
    return jnp.sum(jnp.where(same, row, 0.0), axis=1, keepdims=True)


def as_row(column):
    size = column.shape[0]
    shape = (size, size)
    same = lax.broadcasted_iota(jnp.int32, shape, 0) == lax.broadcasted_iota(jnp.int32, shape, 1)
    return jnp.sum(jnp.where(same, column, 0.0), axis=0, keepdims=True)


def merge(stats):
    highest = jnp.max(stats[:, 0:1, :], axis=0)
    total = jnp.sum(stats[:, 1:2, :] * jnp.exp(stats[:, 0:1, :] - highest[None]), axis=0)
    return highest + jnp.log(total)


def flat_half(blocks):
    count, rows, width = blocks.shape
    return blocks.astype(jnp.float32).reshape(count * rows, width).astype(jnp.bfloat16)


def kernel(
    inner_count,
    line_count,
    pair_count,
    scale_ref,
    image_ref,
    text_ref,
    loss_ref,
    image_grad_ref,
    text_grad_ref,
    images,
    texts,
    row_stats,
    col_stats,
    row_sums,
    col_sums,
    image_parts,
    text_parts,
    image_slots,
    text_slots,
    line_send,
    line_recv,
    plane_send,
    plane_recv,
):
    inner, blk = lax.axis_index("inner"), lax.axis_index("blk")
    place, side = blk // pair_count, lax.rem(blk, pair_count)
    line = Group(
        place, line_count, lambda z: (inner, z * pair_count + side), (line_send, line_recv)
    )
    plane = Group(
        inner * pair_count + side,
        inner_count * pair_count,
        lambda g: (g // pair_count, place * pair_count + lax.rem(g, pair_count)),
        (plane_send, plane_recv),
    )
    groups = (plane, line)
    barrier = pltpu.get_barrier_semaphore()
    for group in groups:
        for step in group.steps():
            pl.semaphore_signal(
                barrier, inc=1, device_id=group.device_of(group.on(step)), device_id_type=MESH
            )

    factor = scale_ref[0]
    image_unit, image_inverse = unit_rows(image_ref[...])
    text_unit, text_inverse = unit_rows(text_ref[...])
    image_half = image_unit.astype(jnp.bfloat16)
    text_half = text_unit.astype(jnp.bfloat16)
    images[line.me] = image_half
    texts[plane.me] = text_half
    pl.semaphore_wait(barrier, plane.size + line.size - 2)
    plane.start_gather(texts, 0)
    line.start_gather(images, 0)
    image_back = image_half.astype(jnp.float32)
    text_back = text_half.astype(jnp.float32)
    diagonal = factor * jnp.sum(image_back * text_back)
    plane.wait_gather(texts, 0)
    line.wait_gather(images, 0)

    image_group = flat_half(images[...])
    text_group = flat_half(texts[...])
    image_count, text_count = image_group.shape[0], text_group.shape[0]
    logits = factor * lax.dot_general(
        image_group, text_group, (((1,), (1,)), ((), ())), preferred_element_type=jnp.float32
    )
    row_peak = jnp.max(logits, axis=1, keepdims=True)
    row_total = jnp.sum(jnp.exp(logits - row_peak), axis=1, keepdims=True)
    col_peak = jnp.max(logits, axis=0, keepdims=True)
    col_total = jnp.sum(jnp.exp(logits - col_peak), axis=0, keepdims=True)
    row_stats[line.me, 0:1, :] = as_row(row_peak)
    row_stats[line.me, 1:2, :] = as_row(row_total)
    col_stats[plane.me, 0:1, :] = col_peak
    col_stats[plane.me, 1:2, :] = col_total
    col_stats[plane.me, 2:3, :] = jnp.full((1, text_count), diagonal, jnp.float32)
    line.start_gather(row_stats, 1)
    plane.start_gather(col_stats, 1)
    line.wait_gather(row_stats, 1)
    plane.wait_gather(col_stats, 1)
    row_lse = merge(row_stats[...])
    col_lse = merge(col_stats[...])

    weights = (
        0.5 * factor * (jnp.exp(logits - as_column(row_lse)) + jnp.exp(logits - col_lse))
    ).astype(jnp.bfloat16)
    text_parts[...] = lax.dot_general(
        weights, image_group, (((0,), (0,)), ((), ())), preferred_element_type=jnp.float32
    ).reshape(text_parts.shape)
    plane.start_scatter(text_parts, text_slots, 2)
    image_parts[...] = jnp.dot(
        weights, text_group, preferred_element_type=jnp.float32
    ).reshape(image_parts.shape)
    line.start_scatter(image_parts, image_slots, 2)

    tile = row_sums.shape[1:]
    plane_diagonal = jnp.sum(col_stats[:, 2, 0:1])
    row_sums[plane.me] = jnp.full(tile, jnp.sum(row_lse), jnp.float32)
    col_sums[line.me] = jnp.full(tile, jnp.sum(col_lse) - 2.0 * plane_diagonal, jnp.float32)
    plane.start_gather(row_sums, 3)
    line.start_gather(col_sums, 3)

    plane.wait_scatter(text_parts, text_slots, 2)
    text_sum = text_parts[plane.me]
    for step in plane.steps():
        text_sum = text_sum + text_slots[step]
    text_grad_ref[...] = project(text_sum - factor * image_back, text_unit, text_inverse)
    line.wait_scatter(image_parts, image_slots, 2)
    image_sum = image_parts[line.me]
    for step in line.steps():
        image_sum = image_sum + image_slots[step]
    image_grad_ref[...] = project(image_sum - factor * text_back, image_unit, image_inverse)

    plane.wait_gather(row_sums, 3)
    line.wait_gather(col_sums, 3)
    examples = 2.0 * line.size * plane.size * image_ref.shape[0]
    whole = jnp.sum(row_sums[...], axis=0)[0, 0] + jnp.sum(col_sums[...], axis=0)[0, 0]
    loss_ref[0] = whole / examples
    for buf_line, buf_plane, stage in (
        (images, texts, 0),
        (row_stats, col_stats, 1),
        (col_sums, row_sums, 3),
    ):
        line.end_gather(buf_line, stage)
        plane.end_gather(buf_plane, stage)


def solution(mesh):
    inner_count, blk_count = mesh.shape["inner"], mesh.shape["blk"]
    pair_count = 2 if blk_count % 2 == 0 else 1
    line_count = blk_count // pair_count
    plane_count = inner_count * pair_count

    def on_device(image_emb, text_emb, logit_scale):
        rows, width = image_emb.shape
        vmem = pl.BlockSpec(memory_space=pltpu.VMEM)
        smem = pl.BlockSpec(memory_space=pltpu.SMEM)
        grad = jax.ShapeDtypeStruct((rows, width), jnp.float32)
        return pl.pallas_call(
            functools.partial(kernel, inner_count, line_count, pair_count),
            out_shape=(jax.ShapeDtypeStruct((1,), jnp.float32), grad, grad),
            in_specs=[smem, vmem, vmem],
            out_specs=(smem, vmem, vmem),
            scratch_shapes=[
                pltpu.VMEM((line_count, rows, width), jnp.bfloat16),
                pltpu.VMEM((plane_count, rows, width), jnp.bfloat16),
                pltpu.VMEM((line_count, 8, line_count * rows), jnp.float32),
                pltpu.VMEM((plane_count, 8, plane_count * rows), jnp.float32),
                pltpu.VMEM((plane_count, 8, 128), jnp.float32),
                pltpu.VMEM((line_count, 8, 128), jnp.float32),
                pltpu.VMEM((line_count, rows, width), jnp.float32),
                pltpu.VMEM((plane_count, rows, width), jnp.float32),
                pltpu.VMEM((line_count, rows, width), jnp.float32),
                pltpu.VMEM((plane_count, rows, width), jnp.float32),
                pltpu.SemaphoreType.DMA((4, line_count)),
                pltpu.SemaphoreType.DMA((4, line_count)),
                pltpu.SemaphoreType.DMA((4, plane_count)),
                pltpu.SemaphoreType.DMA((4, plane_count)),
            ],
            compiler_params=pltpu.CompilerParams(
                collective_id=0, has_side_effects=True, vmem_limit_bytes=56 * 1024 * 1024
            ),
            name="contrastive",
        )(logit_scale, image_emb, text_emb)

    in_specs = (P(("inner", "blk"), None), P(("inner", "blk"), None), P())
    out_specs = (P(), P(("inner", "blk"), None), P(("inner", "blk"), None))
    return jax.shard_map(
        on_device, mesh=mesh, in_specs=in_specs, out_specs=out_specs, check_vma=False
    )
```

```python
import functools

import jax
import jax.numpy as jnp
from jax import lax
from jax.experimental import pallas as pl
from jax.experimental.pallas import tpu as pltpu
from jax.sharding import PartitionSpec as P

EPSILON = 1e-06
MESH = pl.DeviceIdType.MESH


def unit_rows(values):
    inverse = lax.rsqrt(jnp.sum(values * values, axis=1, keepdims=True) + EPSILON)
    return (values * inverse, inverse)


def project(gradient, direction, inverse):
    return (gradient - direction * jnp.sum(gradient * direction, axis=1, keepdims=True)) * inverse


class Group:
    def __init__(self, me, size, device_of, sems):
        self.me, self.size, self.device_of, self.sems = me, size, device_of, sems

    def on(self, step):
        return lax.rem(self.me + step, self.size)

    def back(self, step):
        return lax.rem(self.me + self.size - step, self.size)

    def copy(self, src, dst, stage, step, to):
        send_sems, recv_sems = self.sems
        return pltpu.make_async_remote_copy(
            src_ref=src,
            dst_ref=dst,
            send_sem=send_sems.at[stage, step],
            recv_sem=recv_sems.at[stage, step],
            device_id=self.device_of(to),
            device_id_type=MESH,
        )

    def steps(self):
        return range(1, self.size)

    def start_gather(self, buf, stage):
        mine = buf.at[self.me]
        for step in self.steps():
            self.copy(mine, mine, stage, step, self.on(step)).start()

    def wait_gather(self, buf, stage):
        for step in self.steps():
            theirs = buf.at[self.back(step)]
            self.copy(theirs, theirs, stage, step, self.back(step)).wait_recv()

    def end_gather(self, buf, stage):
        mine = buf.at[self.me]
        for step in self.steps():
            self.copy(mine, mine, stage, step, self.on(step)).wait_send()

    def start_scatter(self, parts, slots, stage):
        for step in self.steps():
            to = self.on(step)
            self.copy(parts.at[to], slots.at[step], stage, step, to).start()

    def wait_scatter(self, parts, slots, stage):
        for step in self.steps():
            to = self.on(step)
            self.copy(parts.at[to], slots.at[step], stage, step, to).wait()


def as_column(row):
    size = row.shape[1]
    shape = (size, size)
    same = lax.broadcasted_iota(jnp.int32, shape, 0) == lax.broadcasted_iota(jnp.int32, shape, 1)
    return jnp.sum(jnp.where(same, row, 0.0), axis=1, keepdims=True)


def as_row(column):
    size = column.shape[0]
    shape = (size, size)
    same = lax.broadcasted_iota(jnp.int32, shape, 0) == lax.broadcasted_iota(jnp.int32, shape, 1)
    return jnp.sum(jnp.where(same, column, 0.0), axis=0, keepdims=True)


def merge(stats):
    highest = jnp.max(stats[:, 0:1, :], axis=0)
    total = jnp.sum(stats[:, 1:2, :] * jnp.exp(stats[:, 0:1, :] - highest[None]), axis=0)
    return highest + jnp.log(total)


def flat_half(blocks):
    count, rows, width = blocks.shape
    return blocks.astype(jnp.float32).reshape(count * rows, width).astype(jnp.bfloat16)


def kernel(
    inner_count,
    line_count,
    pair_count,
    scale_ref,
    image_ref,
    text_ref,
    loss_ref,
    image_grad_ref,
    text_grad_ref,
    images,
    texts,
    row_stats,
    col_stats,
    row_sums,
    col_sums,
    image_parts,
    text_parts,
    image_slots,
    text_slots,
    image_own,
    text_own,
    line_send,
    line_recv,
    plane_send,
    plane_recv,
):
    inner, blk = lax.axis_index("inner"), lax.axis_index("blk")
    place, side = blk // pair_count, lax.rem(blk, pair_count)
    line = Group(
        place, line_count, lambda z: (inner, z * pair_count + side), (line_send, line_recv)
    )
    plane = Group(
        inner * pair_count + side,
        inner_count * pair_count,
        lambda g: (g // pair_count, place * pair_count + lax.rem(g, pair_count)),
        (plane_send, plane_recv),
    )
    groups = (plane, line)
    barrier = pltpu.get_barrier_semaphore()
    for group in groups:
        for step in group.steps():
            pl.semaphore_signal(
                barrier, inc=1, device_id=group.device_of(group.on(step)), device_id_type=MESH
            )

    factor = scale_ref[0]
    image_unit, image_inverse = unit_rows(image_ref[...])
    text_unit, text_inverse = unit_rows(text_ref[...])
    image_half = image_unit.astype(jnp.bfloat16)
    text_half = text_unit.astype(jnp.bfloat16)
    images[line.me] = image_half
    texts[plane.me] = text_half
    pl.semaphore_wait(barrier, plane.size + line.size - 2)
    plane.start_gather(texts, 0)
    line.start_gather(images, 0)
    image_back = image_half.astype(jnp.float32)
    text_back = text_half.astype(jnp.float32)
    diagonal = factor * jnp.sum(image_back * text_back)
    plane.wait_gather(texts, 0)
    line.wait_gather(images, 0)

    image_group = flat_half(images[...])
    text_group = flat_half(texts[...])
    image_count, text_count = image_group.shape[0], text_group.shape[0]
    logits = factor * lax.dot_general(
        image_group, text_group, (((1,), (1,)), ((), ())), preferred_element_type=jnp.float32
    )
    row_peak = jnp.max(logits, axis=1, keepdims=True)
    row_total = jnp.sum(jnp.exp(logits - row_peak), axis=1, keepdims=True)
    col_peak = jnp.max(logits, axis=0, keepdims=True)
    col_total = jnp.sum(jnp.exp(logits - col_peak), axis=0, keepdims=True)
    row_stats[line.me, 0:1, :] = as_row(row_peak)
    row_stats[line.me, 1:2, :] = as_row(row_total)
    col_stats[plane.me, 0:1, :] = col_peak
    col_stats[plane.me, 1:2, :] = col_total
    col_stats[plane.me, 2:3, :] = jnp.full((1, text_count), diagonal, jnp.float32)
    line.start_gather(row_stats, 1)
    plane.start_gather(col_stats, 1)
    line.wait_gather(row_stats, 1)
    plane.wait_gather(col_stats, 1)
    row_lse = merge(row_stats[...])
    col_lse = merge(col_stats[...])

    weights = (
        0.5 * factor * (jnp.exp(logits - as_column(row_lse)) + jnp.exp(logits - col_lse))
    ).astype(jnp.bfloat16)
    text_own[...] = lax.dot_general(
        weights, image_group, (((0,), (0,)), ((), ())), preferred_element_type=jnp.float32
    ).reshape(text_parts.shape)
    text_parts[...] = text_own[...].astype(jnp.bfloat16)
    plane.start_scatter(text_parts, text_slots, 2)
    image_own[...] = jnp.dot(
        weights, text_group, preferred_element_type=jnp.float32
    ).reshape(image_parts.shape)
    image_parts[...] = image_own[...].astype(jnp.bfloat16)
    line.start_scatter(image_parts, image_slots, 2)

    tile = row_sums.shape[1:]
    plane_diagonal = jnp.sum(col_stats[:, 2, 0:1])
    row_sums[plane.me] = jnp.full(tile, jnp.sum(row_lse), jnp.float32)
    col_sums[line.me] = jnp.full(tile, jnp.sum(col_lse) - 2.0 * plane_diagonal, jnp.float32)
    plane.start_gather(row_sums, 3)
    line.start_gather(col_sums, 3)

    plane.wait_scatter(text_parts, text_slots, 2)
    text_sum = text_own[plane.me]
    for step in plane.steps():
        text_sum = text_sum + text_slots[step].astype(jnp.float32)
    text_grad_ref[...] = project(text_sum - factor * image_back, text_unit, text_inverse)
    line.wait_scatter(image_parts, image_slots, 2)
    image_sum = image_own[line.me]
    for step in line.steps():
        image_sum = image_sum + image_slots[step].astype(jnp.float32)
    image_grad_ref[...] = project(image_sum - factor * text_back, image_unit, image_inverse)

    plane.wait_gather(row_sums, 3)
    line.wait_gather(col_sums, 3)
    examples = 2.0 * line.size * plane.size * image_ref.shape[0]
    whole = jnp.sum(row_sums[...], axis=0)[0, 0] + jnp.sum(col_sums[...], axis=0)[0, 0]
    loss_ref[0] = whole / examples
    for buf_line, buf_plane, stage in (
        (images, texts, 0),
        (row_stats, col_stats, 1),
        (col_sums, row_sums, 3),
    ):
        line.end_gather(buf_line, stage)
        plane.end_gather(buf_plane, stage)


def solution(mesh):
    inner_count, blk_count = mesh.shape["inner"], mesh.shape["blk"]
    pair_count = 2 if blk_count % 2 == 0 else 1
    line_count = blk_count // pair_count
    plane_count = inner_count * pair_count

    def on_device(image_emb, text_emb, logit_scale):
        rows, width = image_emb.shape
        vmem = pl.BlockSpec(memory_space=pltpu.VMEM)
        smem = pl.BlockSpec(memory_space=pltpu.SMEM)
        grad = jax.ShapeDtypeStruct((rows, width), jnp.float32)
        return pl.pallas_call(
            functools.partial(kernel, inner_count, line_count, pair_count),
            out_shape=(jax.ShapeDtypeStruct((1,), jnp.float32), grad, grad),
            in_specs=[smem, vmem, vmem],
            out_specs=(smem, vmem, vmem),
            scratch_shapes=[
                pltpu.VMEM((line_count, rows, width), jnp.bfloat16),
                pltpu.VMEM((plane_count, rows, width), jnp.bfloat16),
                pltpu.VMEM((line_count, 8, line_count * rows), jnp.float32),
                pltpu.VMEM((plane_count, 8, plane_count * rows), jnp.float32),
                pltpu.VMEM((plane_count, 8, 128), jnp.float32),
                pltpu.VMEM((line_count, 8, 128), jnp.float32),
                pltpu.VMEM((line_count, rows, width), jnp.bfloat16),
                pltpu.VMEM((plane_count, rows, width), jnp.bfloat16),
                pltpu.VMEM((line_count, rows, width), jnp.bfloat16),
                pltpu.VMEM((plane_count, rows, width), jnp.bfloat16),
                pltpu.VMEM((line_count, rows, width), jnp.float32),
                pltpu.VMEM((plane_count, rows, width), jnp.float32),
                pltpu.SemaphoreType.DMA((4, line_count)),
                pltpu.SemaphoreType.DMA((4, line_count)),
                pltpu.SemaphoreType.DMA((4, plane_count)),
                pltpu.SemaphoreType.DMA((4, plane_count)),
            ],
            compiler_params=pltpu.CompilerParams(
                collective_id=0, has_side_effects=True, vmem_limit_bytes=56 * 1024 * 1024
            ),
            name="contrastive",
        )(logit_scale, image_emb, text_emb)

    in_specs = (P(("inner", "blk"), None), P(("inner", "blk"), None), P())
    out_specs = (P(), P(("inner", "blk"), None), P(("inner", "blk"), None))
    return jax.shard_map(
        on_device, mesh=mesh, in_specs=in_specs, out_specs=out_specs, check_vma=False
    )
```

```python
import functools

import jax
import jax.numpy as jnp
from jax import lax
from jax.experimental import pallas as pl
from jax.experimental.pallas import tpu as pltpu
from jax.sharding import PartitionSpec as P

EPSILON = 1e-06
MESH = pl.DeviceIdType.MESH


def unit_rows(values):
    inverse = lax.rsqrt(jnp.sum(values * values, axis=1, keepdims=True) + EPSILON)
    return (values * inverse, inverse)


def project(gradient, direction, inverse):
    return (gradient - direction * jnp.sum(gradient * direction, axis=1, keepdims=True)) * inverse


class Group:
    def __init__(self, me, size, device_of, sems):
        self.me, self.size, self.device_of, self.sems = me, size, device_of, sems

    def on(self, step):
        return lax.rem(self.me + step, self.size)

    def back(self, step):
        return lax.rem(self.me + self.size - step, self.size)

    def copy(self, src, dst, stage, step, to):
        send_sems, recv_sems = self.sems
        return pltpu.make_async_remote_copy(
            src_ref=src,
            dst_ref=dst,
            send_sem=send_sems.at[stage, step],
            recv_sem=recv_sems.at[stage, step],
            device_id=self.device_of(to),
            device_id_type=MESH,
        )

    def steps(self):
        return range(1, self.size)

    def start_gather(self, buf, stage):
        mine = buf.at[self.me]
        for step in self.steps():
            self.copy(mine, mine, stage, step, self.on(step)).start()

    def wait_gather(self, buf, stage):
        for step in self.steps():
            theirs = buf.at[self.back(step)]
            self.copy(theirs, theirs, stage, step, self.back(step)).wait_recv()

    def end_gather(self, buf, stage):
        mine = buf.at[self.me]
        for step in self.steps():
            self.copy(mine, mine, stage, step, self.on(step)).wait_send()

    def start_scatter(self, parts, slots, stage):
        for step in self.steps():
            to = self.on(step)
            self.copy(parts.at[to], slots.at[step], stage, step, to).start()

    def wait_scatter(self, parts, slots, stage):
        for step in self.steps():
            to = self.on(step)
            self.copy(parts.at[to], slots.at[step], stage, step, to).wait()


def as_column(row):
    size = row.shape[1]
    shape = (size, size)
    same = lax.broadcasted_iota(jnp.int32, shape, 0) == lax.broadcasted_iota(jnp.int32, shape, 1)
    return jnp.sum(jnp.where(same, row, 0.0), axis=1, keepdims=True)


def as_row(column):
    size = column.shape[0]
    shape = (size, size)
    same = lax.broadcasted_iota(jnp.int32, shape, 0) == lax.broadcasted_iota(jnp.int32, shape, 1)
    return jnp.sum(jnp.where(same, column, 0.0), axis=0, keepdims=True)


def merge(stats):
    highest = jnp.max(stats[:, 0:1, :], axis=0)
    total = jnp.sum(stats[:, 1:2, :] * jnp.exp(stats[:, 0:1, :] - highest[None]), axis=0)
    return highest + jnp.log(total)


def flat_half(blocks):
    count, rows, width = blocks.shape
    return blocks.astype(jnp.float32).reshape(count * rows, width).astype(jnp.bfloat16)


def kernel(
    inner_count,
    line_count,
    pair_count,
    scale_ref,
    image_hbm,
    text_hbm,
    loss_ref,
    image_grad_ref,
    text_grad_ref,
    images,
    texts,
    row_stats,
    col_stats,
    row_sums,
    col_sums,
    image_parts,
    text_parts,
    image_slots,
    text_slots,
    image_own,
    text_own,
    image_ref,
    text_ref,
    input_sems,
    line_send,
    line_recv,
    plane_send,
    plane_recv,
):
    text_in = pltpu.make_async_copy(text_hbm, text_ref, input_sems.at[0])
    image_in = pltpu.make_async_copy(image_hbm, image_ref, input_sems.at[1])
    text_in.start()
    image_in.start()
    inner, blk = lax.axis_index("inner"), lax.axis_index("blk")
    place, side = blk // pair_count, lax.rem(blk, pair_count)
    line = Group(
        place, line_count, lambda z: (inner, z * pair_count + side), (line_send, line_recv)
    )
    plane = Group(
        inner * pair_count + side,
        inner_count * pair_count,
        lambda g: (g // pair_count, place * pair_count + lax.rem(g, pair_count)),
        (plane_send, plane_recv),
    )
    groups = (plane, line)
    barrier = pltpu.get_barrier_semaphore()
    for group in groups:
        for step in group.steps():
            pl.semaphore_signal(
                barrier, inc=1, device_id=group.device_of(group.on(step)), device_id_type=MESH
            )

    factor = scale_ref[0]
    text_in.wait()
    text_unit, text_inverse = unit_rows(text_ref[...])
    text_half = text_unit.astype(jnp.bfloat16)
    texts[plane.me] = text_half
    image_in.wait()
    image_unit, image_inverse = unit_rows(image_ref[...])
    image_half = image_unit.astype(jnp.bfloat16)
    images[line.me] = image_half
    pl.semaphore_wait(barrier, plane.size + line.size - 2)
    plane.start_gather(texts, 0)
    line.start_gather(images, 0)
    image_back = image_half.astype(jnp.float32)
    text_back = text_half.astype(jnp.float32)
    diagonal = factor * jnp.sum(image_back * text_back)
    plane.wait_gather(texts, 0)
    line.wait_gather(images, 0)

    image_group = flat_half(images[...])
    text_group = flat_half(texts[...])
    image_count, text_count = image_group.shape[0], text_group.shape[0]
    logits = factor * lax.dot_general(
        image_group, text_group, (((1,), (1,)), ((), ())), preferred_element_type=jnp.float32
    )
    row_peak = jnp.max(logits, axis=1, keepdims=True)
    row_total = jnp.sum(jnp.exp(logits - row_peak), axis=1, keepdims=True)
    col_peak = jnp.max(logits, axis=0, keepdims=True)
    col_total = jnp.sum(jnp.exp(logits - col_peak), axis=0, keepdims=True)
    row_stats[line.me, 0:1, :] = as_row(row_peak)
    row_stats[line.me, 1:2, :] = as_row(row_total)
    col_stats[plane.me, 0:1, :] = col_peak
    col_stats[plane.me, 1:2, :] = col_total
    col_stats[plane.me, 2:3, :] = jnp.full((1, text_count), diagonal, jnp.float32)
    line.start_gather(row_stats, 1)
    plane.start_gather(col_stats, 1)
    line.wait_gather(row_stats, 1)
    plane.wait_gather(col_stats, 1)
    row_lse = merge(row_stats[...])
    col_lse = merge(col_stats[...])

    tile = row_sums.shape[1:]
    plane_diagonal = jnp.sum(col_stats[:, 2, 0:1])
    row_sums[plane.me] = jnp.full(tile, jnp.sum(row_lse), jnp.float32)
    col_sums[line.me] = jnp.full(tile, jnp.sum(col_lse) - 2.0 * plane_diagonal, jnp.float32)
    plane.start_gather(row_sums, 3)
    line.start_gather(col_sums, 3)

    weights = (
        0.5 * factor * (jnp.exp(logits - as_column(row_lse)) + jnp.exp(logits - col_lse))
    ).astype(jnp.bfloat16)
    text_own[...] = lax.dot_general(
        weights, image_group, (((0,), (0,)), ((), ())), preferred_element_type=jnp.float32
    ).reshape(text_parts.shape)
    text_parts[...] = text_own[...].astype(jnp.bfloat16)
    plane.start_scatter(text_parts, text_slots, 2)
    image_own[...] = jnp.dot(
        weights, text_group, preferred_element_type=jnp.float32
    ).reshape(image_parts.shape)
    image_parts[...] = image_own[...].astype(jnp.bfloat16)
    line.start_scatter(image_parts, image_slots, 2)

    plane.wait_scatter(text_parts, text_slots, 2)
    text_sum = text_own[plane.me]
    for step in plane.steps():
        text_sum = text_sum + text_slots[step].astype(jnp.float32)
    text_grad_ref[...] = project(text_sum - factor * image_back, text_unit, text_inverse)
    line.wait_scatter(image_parts, image_slots, 2)
    image_sum = image_own[line.me]
    for step in line.steps():
        image_sum = image_sum + image_slots[step].astype(jnp.float32)
    image_grad_ref[...] = project(image_sum - factor * text_back, image_unit, image_inverse)

    plane.wait_gather(row_sums, 3)
    line.wait_gather(col_sums, 3)
    examples = 2.0 * line.size * plane.size * image_ref.shape[0]
    whole = jnp.sum(row_sums[...], axis=0)[0, 0] + jnp.sum(col_sums[...], axis=0)[0, 0]
    loss_ref[0] = whole / examples
    for buf_line, buf_plane, stage in (
        (images, texts, 0),
        (row_stats, col_stats, 1),
        (col_sums, row_sums, 3),
    ):
        line.end_gather(buf_line, stage)
        plane.end_gather(buf_plane, stage)


def solution(mesh):
    inner_count, blk_count = mesh.shape["inner"], mesh.shape["blk"]
    pair_count = 2 if blk_count % 2 == 0 else 1
    line_count = blk_count // pair_count
    plane_count = inner_count * pair_count

    def on_device(image_emb, text_emb, logit_scale):
        rows, width = image_emb.shape
        vmem = pl.BlockSpec(memory_space=pltpu.VMEM)
        hbm = pl.BlockSpec(memory_space=pl.ANY)
        smem = pl.BlockSpec(memory_space=pltpu.SMEM)
        near = pltpu.VMEM((rows, width), jnp.float32)
        return pl.pallas_call(
            functools.partial(kernel, inner_count, line_count, pair_count),
            out_shape=(jax.ShapeDtypeStruct((1,), jnp.float32), near, near),
            in_specs=[smem, hbm, hbm],
            out_specs=(smem, vmem, vmem),
            scratch_shapes=[
                pltpu.VMEM((line_count, rows, width), jnp.bfloat16),
                pltpu.VMEM((plane_count, rows, width), jnp.bfloat16),
                pltpu.VMEM((line_count, 2, line_count * rows), jnp.float32),
                pltpu.VMEM((plane_count, 4, plane_count * rows), jnp.float32),
                pltpu.VMEM((plane_count, 1, 128), jnp.float32),
                pltpu.VMEM((line_count, 1, 128), jnp.float32),
                pltpu.VMEM((line_count, rows, width), jnp.bfloat16),
                pltpu.VMEM((plane_count, rows, width), jnp.bfloat16),
                pltpu.VMEM((line_count, rows, width), jnp.bfloat16),
                pltpu.VMEM((plane_count, rows, width), jnp.bfloat16),
                pltpu.VMEM((line_count, rows, width), jnp.float32),
                pltpu.VMEM((plane_count, rows, width), jnp.float32),
                pltpu.VMEM((rows, width), jnp.float32),
                pltpu.VMEM((rows, width), jnp.float32),
                pltpu.SemaphoreType.DMA((2,)),
                pltpu.SemaphoreType.DMA((4, line_count)),
                pltpu.SemaphoreType.DMA((4, line_count)),
                pltpu.SemaphoreType.DMA((4, plane_count)),
                pltpu.SemaphoreType.DMA((4, plane_count)),
            ],
            compiler_params=pltpu.CompilerParams(
                collective_id=0, has_side_effects=True, vmem_limit_bytes=56 * 1024 * 1024
            ),
            name="contrastive",
        )(logit_scale, image_emb, text_emb)

    in_specs = (P(("inner", "blk"), None), P(("inner", "blk"), None), P())
    out_specs = (P(), P(("inner", "blk"), None), P(("inner", "blk"), None))
    return jax.shard_map(
        on_device, mesh=mesh, in_specs=in_specs, out_specs=out_specs, check_vma=False
    )
```

```python
import functools

import jax
import jax.numpy as jnp
from jax import lax
from jax.experimental import pallas as pl
from jax.experimental.pallas import tpu as pltpu
from jax.sharding import PartitionSpec as P

EPSILON = 1e-06
MESH = pl.DeviceIdType.MESH


def unit_rows(values):
    inverse = lax.rsqrt(jnp.sum(values * values, axis=1, keepdims=True) + EPSILON)
    return (values * inverse, inverse)


def project(gradient, direction, inverse):
    return (gradient - direction * jnp.sum(gradient * direction, axis=1, keepdims=True)) * inverse


class Group:
    def __init__(self, me, size, device_of, sems):
        self.me, self.size, self.device_of, self.sems = me, size, device_of, sems

    def on(self, step):
        return lax.rem(self.me + step, self.size)

    def back(self, step):
        return lax.rem(self.me + self.size - step, self.size)

    def copy(self, src, dst, stage, step, to):
        send_sems, recv_sems = self.sems
        return pltpu.make_async_remote_copy(
            src_ref=src,
            dst_ref=dst,
            send_sem=send_sems.at[stage, step],
            recv_sem=recv_sems.at[stage, step],
            device_id=self.device_of(to),
            device_id_type=MESH,
        )

    def steps(self):
        return range(1, self.size)

    def start_gather(self, buf, stage):
        mine = buf.at[self.me]
        for step in self.steps():
            self.copy(mine, mine, stage, step, self.on(step)).start()

    def wait_gather(self, buf, stage):
        for step in self.steps():
            theirs = buf.at[self.back(step)]
            self.copy(theirs, theirs, stage, step, self.back(step)).wait_recv()

    def end_gather(self, buf, stage):
        mine = buf.at[self.me]
        for step in self.steps():
            self.copy(mine, mine, stage, step, self.on(step)).wait_send()

    def start_scatter(self, parts, slots, stage):
        for step in self.steps():
            to = self.on(step)
            self.copy(parts.at[to], slots.at[step], stage, step, to).start()

    def wait_scatter(self, parts, slots, stage):
        for step in self.steps():
            to = self.on(step)
            self.copy(parts.at[to], slots.at[step], stage, step, to).wait()


def as_column(row):
    size = row.shape[1]
    shape = (size, size)
    same = lax.broadcasted_iota(jnp.int32, shape, 0) == lax.broadcasted_iota(jnp.int32, shape, 1)
    return jnp.sum(jnp.where(same, row, 0.0), axis=1, keepdims=True)


def as_row(column):
    size = column.shape[0]
    shape = (size, size)
    same = lax.broadcasted_iota(jnp.int32, shape, 0) == lax.broadcasted_iota(jnp.int32, shape, 1)
    return jnp.sum(jnp.where(same, column, 0.0), axis=0, keepdims=True)


def merge(stats):
    highest = jnp.max(stats[:, 0:1, :], axis=0)
    total = jnp.sum(stats[:, 1:2, :] * jnp.exp(stats[:, 0:1, :] - highest[None]), axis=0)
    return highest + jnp.log(total)


def flat_half(blocks):
    count, rows, width = blocks.shape
    return blocks.astype(jnp.float32).reshape(count * rows, width).astype(jnp.bfloat16)


def kernel(
    inner_count,
    line_count,
    pair_count,
    scale_ref,
    image_hbm,
    text_hbm,
    loss_ref,
    image_grad_ref,
    text_grad_ref,
    images,
    texts,
    row_stats,
    col_stats,
    row_sums,
    col_sums,
    image_parts,
    text_parts,
    image_slots,
    text_slots,
    image_own,
    text_own,
    image_ref,
    text_ref,
    input_sems,
    line_send,
    line_recv,
    plane_send,
    plane_recv,
):
    text_in = pltpu.make_async_copy(text_hbm, text_ref, input_sems.at[0])
    image_in = pltpu.make_async_copy(image_hbm, image_ref, input_sems.at[1])
    text_in.start()
    image_in.start()
    inner, blk = lax.axis_index("inner"), lax.axis_index("blk")
    place, side = blk // pair_count, lax.rem(blk, pair_count)
    line = Group(
        place, line_count, lambda z: (inner, z * pair_count + side), (line_send, line_recv)
    )
    plane = Group(
        inner * pair_count + side,
        inner_count * pair_count,
        lambda g: (g // pair_count, place * pair_count + lax.rem(g, pair_count)),
        (plane_send, plane_recv),
    )
    groups = (plane, line)
    barrier = pltpu.get_barrier_semaphore()
    for group in groups:
        for step in group.steps():
            pl.semaphore_signal(
                barrier, inc=1, device_id=group.device_of(group.on(step)), device_id_type=MESH
            )

    factor = scale_ref[0]
    text_in.wait()
    text_unit, text_inverse = unit_rows(text_ref[...])
    text_half = text_unit.astype(jnp.bfloat16)
    texts[plane.me] = text_half
    image_in.wait()
    image_unit, image_inverse = unit_rows(image_ref[...])
    image_half = image_unit.astype(jnp.bfloat16)
    images[line.me] = image_half
    pl.semaphore_wait(barrier, plane.size + line.size - 2)
    line.start_gather(images, 0)
    plane.start_gather(texts, 0)
    image_back = image_half.astype(jnp.float32)
    text_back = text_half.astype(jnp.float32)
    diagonal = factor * jnp.sum(image_back * text_back)
    plane.wait_gather(texts, 0)
    line.wait_gather(images, 0)

    image_group = flat_half(images[...])
    text_group = flat_half(texts[...])
    image_count, text_count = image_group.shape[0], text_group.shape[0]
    logits = factor * lax.dot_general(
        image_group, text_group, (((1,), (1,)), ((), ())), preferred_element_type=jnp.float32
    )
    row_peak = jnp.max(logits, axis=1, keepdims=True)
    row_total = jnp.sum(jnp.exp(logits - row_peak), axis=1, keepdims=True)
    col_peak = jnp.max(logits, axis=0, keepdims=True)
    col_total = jnp.sum(jnp.exp(logits - col_peak), axis=0, keepdims=True)
    row_stats[line.me, 0:1, :] = as_row(row_peak)
    row_stats[line.me, 1:2, :] = as_row(row_total)
    col_stats[plane.me, 0:1, :] = col_peak
    col_stats[plane.me, 1:2, :] = col_total
    col_stats[plane.me, 2:3, :] = jnp.full((1, text_count), diagonal, jnp.float32)
    line.start_gather(row_stats, 1)
    plane.start_gather(col_stats, 1)
    line.wait_gather(row_stats, 1)
    plane.wait_gather(col_stats, 1)
    row_lse = merge(row_stats[...])
    col_lse = merge(col_stats[...])

    tile = row_sums.shape[1:]
    plane_diagonal = jnp.sum(col_stats[:, 2, 0:1])
    row_sums[plane.me] = jnp.full(tile, jnp.sum(row_lse), jnp.float32)
    col_sums[line.me] = jnp.full(tile, jnp.sum(col_lse) - 2.0 * plane_diagonal, jnp.float32)
    plane.start_gather(row_sums, 3)
    line.start_gather(col_sums, 3)

    weights = (
        0.5 * factor * (jnp.exp(logits - as_column(row_lse)) + jnp.exp(logits - col_lse))
    ).astype(jnp.bfloat16)
    image_own[...] = jnp.dot(
        weights, text_group, preferred_element_type=jnp.float32
    ).reshape(image_parts.shape)
    image_parts[...] = image_own[...].astype(jnp.bfloat16)
    line.start_scatter(image_parts, image_slots, 2)
    text_own[...] = lax.dot_general(
        weights, image_group, (((0,), (0,)), ((), ())), preferred_element_type=jnp.float32
    ).reshape(text_parts.shape)
    text_parts[...] = text_own[...].astype(jnp.bfloat16)
    plane.start_scatter(text_parts, text_slots, 2)

    plane.wait_scatter(text_parts, text_slots, 2)
    text_sum = text_own[plane.me]
    for step in plane.steps():
        text_sum = text_sum + text_slots[step].astype(jnp.float32)
    text_grad_ref[...] = project(text_sum - factor * image_back, text_unit, text_inverse)
    line.wait_scatter(image_parts, image_slots, 2)
    image_sum = image_own[line.me]
    for step in line.steps():
        image_sum = image_sum + image_slots[step].astype(jnp.float32)
    image_grad_ref[...] = project(image_sum - factor * text_back, image_unit, image_inverse)

    plane.wait_gather(row_sums, 3)
    line.wait_gather(col_sums, 3)
    examples = 2.0 * line.size * plane.size * image_ref.shape[0]
    whole = jnp.sum(row_sums[...], axis=0)[0, 0] + jnp.sum(col_sums[...], axis=0)[0, 0]
    loss_ref[0] = whole / examples
    for buf_line, buf_plane, stage in (
        (images, texts, 0),
        (row_stats, col_stats, 1),
        (col_sums, row_sums, 3),
    ):
        line.end_gather(buf_line, stage)
        plane.end_gather(buf_plane, stage)


def solution(mesh):
    inner_count, blk_count = mesh.shape["inner"], mesh.shape["blk"]
    pair_count = 2 if blk_count % 2 == 0 else 1
    line_count = blk_count // pair_count
    plane_count = inner_count * pair_count

    def on_device(image_emb, text_emb, logit_scale):
        rows, width = image_emb.shape
        vmem = pl.BlockSpec(memory_space=pltpu.VMEM)
        hbm = pl.BlockSpec(memory_space=pl.ANY)
        smem = pl.BlockSpec(memory_space=pltpu.SMEM)
        near = pltpu.VMEM((rows, width), jnp.float32)
        return pl.pallas_call(
            functools.partial(kernel, inner_count, line_count, pair_count),
            out_shape=(jax.ShapeDtypeStruct((1,), jnp.float32), near, near),
            in_specs=[smem, hbm, hbm],
            out_specs=(smem, vmem, vmem),
            scratch_shapes=[
                pltpu.VMEM((line_count, rows, width), jnp.bfloat16),
                pltpu.VMEM((plane_count, rows, width), jnp.bfloat16),
                pltpu.VMEM((line_count, 2, line_count * rows), jnp.float32),
                pltpu.VMEM((plane_count, 4, plane_count * rows), jnp.float32),
                pltpu.VMEM((plane_count, 1, 128), jnp.float32),
                pltpu.VMEM((line_count, 1, 128), jnp.float32),
                pltpu.VMEM((line_count, rows, width), jnp.bfloat16),
                pltpu.VMEM((plane_count, rows, width), jnp.bfloat16),
                pltpu.VMEM((line_count, rows, width), jnp.bfloat16),
                pltpu.VMEM((plane_count, rows, width), jnp.bfloat16),
                pltpu.VMEM((line_count, rows, width), jnp.float32),
                pltpu.VMEM((plane_count, rows, width), jnp.float32),
                pltpu.VMEM((rows, width), jnp.float32),
                pltpu.VMEM((rows, width), jnp.float32),
                pltpu.SemaphoreType.DMA((2,)),
                pltpu.SemaphoreType.DMA((4, line_count)),
                pltpu.SemaphoreType.DMA((4, line_count)),
                pltpu.SemaphoreType.DMA((4, plane_count)),
                pltpu.SemaphoreType.DMA((4, plane_count)),
            ],
            compiler_params=pltpu.CompilerParams(
                collective_id=0, has_side_effects=True, vmem_limit_bytes=56 * 1024 * 1024
            ),
            name="contrastive",
        )(logit_scale, image_emb, text_emb)

    in_specs = (P(("inner", "blk"), None), P(("inner", "blk"), None), P())
    out_specs = (P(), P(("inner", "blk"), None), P(("inner", "blk"), None))
    return jax.shard_map(
        on_device, mesh=mesh, in_specs=in_specs, out_specs=out_specs, check_vma=False
    )
```
